128 devices in a mesh: batch: 4 (over z_hi, core), ctx: 32 (over z_lo, y, x).
Axes of the slice: x: 4, y: 4, z: 4 (z_hi: 2, z_lo: 2; z = z_hi * 2 + z_lo), core: 2. Of those that a mesh axis runs over, the one named last changes fastest.
Arguments:
- lengths: int32 [64], P('batch'), parts along dimension 0, may hold values from 1 to 8704, 16384 in all
- queries: bfloat16 [65536, 512], P(('batch', 'ctx')), parts along dimension 0, may hold values from -256 to 256
- key_rows: bfloat16 [65536, 128], P(('batch', 'ctx')), parts along dimension 0, may hold values from -4.5 to 4.5
- values: bfloat16 [65536, 128], P(('batch', 'ctx')), parts along dimension 0, may hold values from -6 to 6
Outputs:
- attended: bfloat16 [65536, 512], P(('batch', 'ctx')), parts along dimension 0
- log_mass: float32 [4, 65536], P(None, ('batch', 'ctx')), parts along dimension 1
The draws below stay inside these ranges and needn't reach their ends.
There are 4 independent parts, one for each index of `batch`. The reference program is written for one: setup_inputs(seed, part) draws one part's arguments, and reference() takes and returns one part's arrays. A program takes and returns all parts, laid end to end along the dimension named above; each array names one. Nothing has to cross between parts.
Inputs may be any that keep to these rules, and one draw needn't show every extreme that they name: The lengths sum to 16384; the longest is exactly 8704.
All inputs are finite; a program needn't handle non-finite values.
Results may differ from the reference program's by a relative error of at most 0.0035.
Values may be sent and summed in bfloat16 or wider, within the bound.
A program may use at most 64 MiB of HBM per device.

```python
import math
import jax
import jax.numpy as jnp
import numpy as np
from jax import lax

QH = 4
HD = 128
DOCS = 16
SEQ = 16384
MOST = 8704


def drawn_keys(key):
    seeded = jax.random.fold_in(key, 17)
    drawn = jnp.clip(jax.random.normal(seeded, (SEQ, HD), jnp.float32), -4.5, 4.5)
    return drawn


def draw_key_rows(key, part):
    return drawn_keys(key).astype(jnp.bfloat16)


def draw_queries(key, part):
    seeded = jax.random.fold_in(key, 23)
    background = jnp.clip(1.5 * jax.random.normal(seeded, (SEQ, QH * HD), jnp.float32), -9.0, 9.0)
    return background.astype(jnp.bfloat16)


def block_scale(rng, dims, shards, least, largest):
    def one(dim, blocks):
        heights = jax.random.uniform(jax.random.fold_in(jax.random.fold_in(rng, 6), dim), (blocks,), jnp.float32, least / len(shards), largest / len(shards))
        return jnp.repeat(jnp.exp(heights), dims[dim] // blocks).reshape((-1,) + (1,) * (len(dims) - dim - 1))

    loudness = one(*shards[0])
    for cut in shards[1:]:
        loudness = loudness * one(*cut)
    return loudness


def length_profile(count, total, most, lean):
    loads = [(1 << 20) // math.isqrt(standing ** lean) + 1 for standing in range(2, count + 1)]
    spare, counts = total - most - (count - 1), [1] * (count - 1)
    while spare > 0:
        movable = [i for i in range(count - 1) if counts[i] < most]
        pool, remaining = sum([loads[i] for i in movable]), spare
        for i in movable:
            extra = min(most - counts[i], max(1, remaining * loads[i] // pool), spare)
            counts[i] = counts[i] + extra
            spare = spare - extra
    return np.array([most] + counts)


def uneven_parts(stream_key, number_of, total, reach, skew):
    if number_of == 2:
        one = jax.random.randint(stream_key, (), max(1, total - reach), min(reach, total - 1) + 1)
        return jnp.stack([one, total - one])
    sizes = jnp.asarray(length_profile(number_of, total, reach, skew), jnp.int32)
    twos = (number_of - 1) // 2
    source_of, sink = sizes[1:1 + 2 * twos:2], sizes[2:2 + 2 * twos:2]
    margin = jnp.minimum(source_of - 1, reach - sink)
    shifted = jax.random.randint(jax.random.fold_in(stream_key, 1), (twos,), 0, 1 << 20) % (margin + 1)
    sizes = sizes.at[1:1 + 2 * twos:2].set(source_of - shifted).at[2:2 + 2 * twos:2].set(sink + shifted)
    return sizes[jax.random.permutation(jax.random.fold_in(stream_key, 2), number_of)]


def gaussian(stream_key, dims, scale, bound, pieces=(), held_as=jnp.bfloat16):
    result = jax.random.normal(stream_key, dims, jnp.float32) * scale
    if len(pieces) > 0:
        result = block_scale(stream_key, dims, pieces, -0.22, 0.18) * result
    return jnp.clip(result, min=-bound, max=bound).astype(held_as)


def setup_inputs(seed: int = 0, part: int = 0) -> dict:
    seeds = jax.random.split(jax.random.key(seed), 5)
    part_splits = jax.random.split(jax.random.fold_in(seeds[4], part), 5)
    return {
        "lengths": uneven_parts(part_splits[0], DOCS, SEQ, MOST, 2).astype(jnp.int32),
        "queries": draw_queries(jax.random.fold_in(jax.random.fold_in(seeds[4], part), 71), part),
        "key_rows": draw_key_rows(jax.random.fold_in(jax.random.fold_in(seeds[4], part), 71), part),
        "values": gaussian(part_splits[3], (SEQ, HD), 1.0, 6.0, ((0, 32),)),
    }


def doc_numbers(lengths, positions):
    doc_ends = jnp.cumsum(lengths).astype(jnp.int32)
    return jnp.sum((positions[:, None] >= doc_ends[None, :]).astype(jnp.int32), axis=1)


def reference(lengths, queries, key_rows, values):
    all_pos = jnp.arange(SEQ, dtype=jnp.int32)
    doc_index = doc_numbers(lengths, all_pos)
    block_rows = min(512, SEQ)
    block_count = SEQ // block_rows
    query_blocks = queries.reshape(block_count, block_rows, QH, HD)
    first_rows = (jnp.arange(block_count, dtype=jnp.int32) * block_rows).astype(jnp.int32)
    score_scale = 1.0 / (HD ** 0.5)
    keys_wide = key_rows.astype(jnp.float32)
    values_wide = values.astype(jnp.float32)

    def attend_block(packed):
        query_block, first_row = packed
        q_pos = first_row + jnp.arange(block_rows, dtype=jnp.int32)
        q_doc = lax.dynamic_slice_in_dim(doc_index, first_row, block_rows, 0)
        visible = (q_doc[:, None] == doc_index[None, :]) & (all_pos[None, :] <= q_pos[:, None])
        scores = jnp.einsum('thd,kd->htk', query_block.astype(jnp.float32), keys_wide) * score_scale
        scores = jnp.where(visible[None], scores, -1e30)
        row_max = jnp.max(scores, axis=2)
        weights = jnp.where(visible[None], jnp.exp(scores - row_max[:, :, None]), 0.0)
        total = jnp.sum(weights, axis=2)
        weight_bf = weights.astype(jnp.bfloat16)
        mixed = jnp.einsum('htk,kd->thd', weight_bf.astype(jnp.float32), values_wide)
        mixed = mixed / jnp.transpose(total)[:, :, None]
        attended = mixed.reshape(block_rows, QH * HD).astype(jnp.bfloat16)
        return attended, row_max + jnp.log(total)

    attended, log_mass = lax.map(attend_block, (query_blocks, first_rows))
    attended = attended.reshape(SEQ, QH * HD)
    log_mass = jnp.transpose(log_mass, (1, 0, 2)).reshape(QH, SEQ)
    return attended, log_mass
```

```python
import math

import jax
import jax.numpy as jnp
from jax import lax
from jax.experimental import pallas as pl
from jax.experimental.pallas import tpu as pltpu
from jax.sharding import PartitionSpec as P

QH = 4
HD = 128
DOCS = 16
ROWS = 512
PAIR = 2 * ROWS
CHUNK = 512
STRIP = 64
FAR = 1 << 20
HIDE = float(2**20)
SCALE = 1.0 / math.sqrt(HD)
TO_TWO = SCALE / math.log(2.0)
MESH = pl.DeviceIdType.MESH

SWAP, PRED, OWN = 0, 16, 17
SLOT = {
    (3, 0): 1,
    (0, 3): 2,
    (3, 3): 3,
    (1, 0): 4,
    (0, 1): 5,
    (2, 0): 6,
    (3, 1): 7,
    (1, 3): 8,
    (2, 3): 9,
    (1, 1): 10,
    (2, 1): 11,
    (0, 2): 12,
    (3, 2): 13,
    (1, 2): 14,
    (2, 2): 15,
}
AT = {slot: column for column, slot in SLOT.items()}
SENDS = 18


def body(lengths, queries, keys, values, attended, log_mass, kv, qa, acc, top, scores, weights, feats, docs, local, sent, got):
    here = lax.axis_index("ctx")
    z, y, x = here // 16, here // 4 % 4, here % 4
    at_x = lambda to: z * 16 + y * 4 + to % 4
    at_y = lambda to: z * 16 + to % 4 * 4 + x
    left, right, up, down = at_x(x + 3), at_x(x + 1), at_y(y + 3), at_y(y + 1)
    other = (1 - z) * 16 + y * 4 + x

    own_copies = [
        pltpu.make_async_copy(keys, kv.at[OWN // 2, 0, pl.ds(ROWS, ROWS)], local.at[0]),
        pltpu.make_async_copy(values, kv.at[OWN // 2, 1, pl.ds(ROWS, ROWS)], local.at[1]),
    ]
    for copy in own_copies:
        copy.start()
    barrier = pltpu.get_barrier_semaphore()
    for neighbour in (left, right, up, down, other):
        pl.semaphore_signal(barrier, inc=1, device_id={"ctx": neighbour}, device_id_type=MESH)
    pl.semaphore_wait(barrier, 5)
    for copy in own_copies:
        copy.wait()

    def held(slot):
        return kv.at[slot // 2, :, pl.ds(slot % 2 * ROWS, ROWS)]

    def push(number, source, slot, to):
        return pltpu.make_async_remote_copy(
            src_ref=held(source),
            dst_ref=held(slot),
            send_sem=sent.at[number],
            recv_sem=got.at[slot],
            device_id={"ctx": to},
            device_id_type=MESH,
        )

    def arrive(slot):
        push(0, OWN, slot, other).wait_recv()

    firsts = (
        (1, SLOT[0, 3], right, x < 3),
        (2, SLOT[0, 1], left, x == 0),
        (3, SLOT[3, 0], down, y < 3),
        (4, SLOT[1, 0], up, y == 0),
    )
    middle_x = (x == 1) | (x == 2)
    middle_y = (y == 1) | (y == 2)

    push(0, OWN, SWAP, other).start()
    for number, slot, to, later in firsts:

        @pl.when(later | (z == 0))
        def _():
            push(number, OWN, slot, to).start()

    lane = lax.broadcasted_iota(jnp.int32, (8, 128), 1)
    begins, ends = jnp.full((8, 128), FAR, jnp.int32), jnp.zeros((8, 128), jnp.int32)
    total = jnp.int32(0)
    for doc in range(DOCS):
        begins = jnp.where(lane == doc, total, begins)
        total = total + lengths[doc]
        ends = jnp.where(lane == doc, total, ends)
    docs[0:8] = begins
    docs[8:16] = ends

    def inside(first):
        place = first + lax.broadcasted_iota(jnp.int32, (ROWS, 128), 0)
        return (place >= docs[0:1]) & (place < docs[8:9])

    hide = jnp.where(inside(here * ROWS), -HIDE, 0.0).astype(jnp.bfloat16)
    for head in range(QH):
        qa[head * ROWS : (head + 1) * ROWS, 0:HD] = queries[:, head * HD : (head + 1) * HD]
        qa[head * ROWS : (head + 1) * ROWS, HD:] = hide
    top[...] = jnp.full(top.shape, -1e30, jnp.float32)
    acc[...] = jnp.zeros(acc.shape, jnp.float32)

    def attend(pair, half, width, reach):
        where = pl.ds(half * ROWS, width)
        key_part = jnp.concatenate([kv[pair, 0, where], feats[where]], 1)
        value_part = jnp.concatenate([kv[pair, 1, where], jnp.ones((width, HD), jnp.bfloat16)], 1)
        chunks = QH * ROWS // CHUNK

        def score(chunk):
            scores[chunk % 2, :, 0:width] = lax.dot_general(
                qa[chunk * CHUNK : (chunk + 1) * CHUNK],
                key_part,
                (((1,), (1,)), ((), ())),
                preferred_element_type=jnp.float32,
            )

        def soften(chunk):
            for strip in range(CHUNK // STRIP):
                at = slice(strip * STRIP, (strip + 1) * STRIP)
                rows = slice(chunk * CHUNK + strip * STRIP, chunk * CHUNK + (strip + 1) * STRIP)
                raw = scores[chunk % 2, at, 0:width]
                if reach is not None:
                    row = rows.start % ROWS + lax.broadcasted_iota(jnp.int32, raw.shape, 0)
                    raw = jnp.where(lax.broadcasted_iota(jnp.int32, raw.shape, 1) <= row + reach, raw, -1e30)
                parts = [raw[:, j : j + 128] for j in range(0, width, 128)]
                most = parts[0]
                for part in parts[1:]:
                    most = jnp.maximum(most, part)
                most = jnp.broadcast_to(jnp.max(most, axis=1, keepdims=True), (STRIP, 128))
                before = top[rows]
                now = jnp.maximum(before, most)
                fade = jnp.exp2((before - now) * TO_TWO)
                acc[rows] = acc[rows] * jnp.concatenate([fade, fade], 1)
                top[rows] = now
                for j, part in enumerate(parts):
                    weights[chunk % 2, at, j * 128 : (j + 1) * 128] = jnp.exp2((part - now) * TO_TWO).astype(
                        jnp.bfloat16
                    )

        def mix(chunk):
            rows = slice(chunk * CHUNK, (chunk + 1) * CHUNK)
            acc[rows] = acc[rows] + jnp.dot(
                weights[chunk % 2, :, 0:width], value_part, preferred_element_type=jnp.float32
            )

        score(0)
        for chunk in range(chunks):
            if chunk + 1 < chunks:
                score(chunk + 1)
            if chunk > 0:
                mix(chunk - 1)
            soften(chunk)
        mix(chunks - 1)

    def first_of(slot):
        if slot == OWN:
            return here * ROWS
        if slot == PRED:
            return jnp.where((z == 1) & (here > 16), (here - 17) * ROWS, FAR)
        if slot == SWAP:
            return jnp.where(z == 1, (here - 16) * ROWS, FAR)
        dy, dx = AT[slot]
        column = (y + dy) % 4 * 4 + (x + dx) % 4
        before = column < here % 16
        return jnp.where(before, z * 16 + column, jnp.where(z == 1, column, FAR // ROWS)) * ROWS

    def look(slot):
        feats[pl.ds(slot % 2 * ROWS, ROWS)] = jnp.where(inside(first_of(slot)), 0.0, 1.0).astype(jnp.bfloat16)

    def onward(slot, number):
        dy, _ = AT[slot]
        push(number, slot, SLOT[dy, 3], right).start()
        push(number + 1, slot, SLOT[dy, 1], left).start()

    def relay(slot, number):
        dy, dx = AT[slot]
        to = right if dx == 3 else left

        @pl.when(middle_x if dy in (0, 1) else ~middle_x)
        def _():
            push(number, slot, SLOT[dy, 2], to).start()

    def before_pair(pair):
        for slot in (2 * pair, 2 * pair + 1):
            arrive(slot)
            if slot == SWAP:
                for number, there, to, later in firsts:

                    @pl.when(~(later | (z == 0)))
                    def _():
                        push(number, SWAP, there, to).start()

            elif slot == SLOT[3, 0]:
                onward(slot, 5)

                @pl.when(middle_y)
                def _():
                    push(11, SLOT[3, 0], SLOT[2, 0], down).start()

            elif slot == SLOT[1, 0]:
                onward(slot, 7)

                @pl.when(middle_y)
                def _():
                    push(12, SLOT[1, 0], SLOT[2, 0], up).start()

            elif slot == SLOT[2, 0]:
                onward(slot, 9)
            elif AT[slot][1] == 3:
                relay(slot, 13 if AT[slot][0] in (0, 3) else 14)
            elif AT[slot][1] == 1:
                relay(slot, 15 if AT[slot][0] in (0, 3) else 16)
            look(slot)
        if pair == 1:
            push(17, jnp.where(x > 0, SLOT[0, 3], SLOT[3, 3]), PRED, other).start()

    def step(number, nothing):
        single = (number == 0) | (number == 7)
        pair = jnp.where(number > 7, number - 2, number - 1)
        for which in range(8):

            @pl.when(~single & (pair == which))
            def _():
                before_pair(which)

        @pl.when(number == 0)
        def _():
            look(OWN)

        @pl.when(number == 7)
        def _():
            arrive(PRED)
            look(PRED)

        @pl.when(single)
        def _():
            half = jnp.where(number == 0, 1, 0)
            attend(OWN // 2, pl.multiple_of(half, 1), ROWS, jnp.where(number == 0, 0, ROWS))

        @pl.when(~single)
        def _():
            attend(pair, 0, PAIR, None)

        return nothing

    lax.fori_loop(0, 10, step, 0)

    for head in range(QH):
        rows = slice(head * ROWS, (head + 1) * ROWS)
        mass = acc[rows, HD : HD + 1]
        attended[:, head * HD : (head + 1) * HD] = (acc[rows, 0:HD] / mass).astype(jnp.bfloat16)
        log_mass[head : head + 1, :] = (top[rows, 0:1] * SCALE + jnp.log(mass)).reshape(1, ROWS)

    for number in range(SENDS):
        if number in (11, 12):

            @pl.when(middle_y)
            def _():
                push(number, OWN, SWAP, other).wait_send()

        else:
            push(number, OWN, SWAP, other).wait_send()


def on_device(lengths, queries, key_rows, values):
    vmem = pl.BlockSpec(memory_space=pltpu.VMEM)
    return pl.pallas_call(
        body,
        out_shape=(
            jax.ShapeDtypeStruct((ROWS, QH * HD), jnp.bfloat16),
            jax.ShapeDtypeStruct((QH, ROWS), jnp.float32),
        ),
        in_specs=[
            pl.BlockSpec(memory_space=pltpu.SMEM),
            vmem,
            pl.BlockSpec(memory_space=pl.ANY),
            pl.BlockSpec(memory_space=pl.ANY),
        ],
        out_specs=(vmem, vmem),
        scratch_shapes=[
            pltpu.VMEM((9, 2, PAIR, HD), jnp.bfloat16),
            pltpu.VMEM((QH * ROWS, 2 * HD), jnp.bfloat16),
            pltpu.VMEM((QH * ROWS, 2 * HD), jnp.float32),
            pltpu.VMEM((QH * ROWS, HD), jnp.float32),
            pltpu.VMEM((2, CHUNK, PAIR), jnp.float32),
            pltpu.VMEM((2, CHUNK, PAIR), jnp.bfloat16),
            pltpu.VMEM((PAIR, HD), jnp.bfloat16),
            pltpu.VMEM((16, 128), jnp.int32),
            pltpu.SemaphoreType.DMA((2,)),
            pltpu.SemaphoreType.DMA((SENDS,)),
            pltpu.SemaphoreType.DMA((OWN,)),
        ],
        compiler_params=pltpu.CompilerParams(collective_id=0, has_side_effects=True, vmem_limit_bytes=56 << 20),
    )(lengths, queries, key_rows, values)


def solution(mesh):
    in_specs = (
        P("batch"),
        P(("batch", "ctx"), None),
        P(("batch", "ctx"), None),
        P(("batch", "ctx"), None),
    )
    out_specs = (P(("batch", "ctx"), None), P(None, ("batch", "ctx")))
    step = jax.shard_map(on_device, mesh=mesh, in_specs=in_specs, out_specs=out_specs, check_vma=False)

    def run(*args):
        with jax.sharding.use_abstract_mesh(mesh.abstract_mesh):
            return step(*args)

    return run
```

```python
import math

import jax
import jax.numpy as jnp
from jax import lax
from jax.experimental import pallas as pl
from jax.experimental.pallas import tpu as pltpu
from jax.sharding import PartitionSpec as P

QH = 4
HD = 128
DOCS = 16
ROWS = 512
PAIR = 2 * ROWS
SHARE = 192
DEPTH = HD + 16
FAR = 1 << 20
HIDE = float(2**20)
LOWEST = -3e38
SCALE = 1.0 / math.sqrt(HD)
TO_TWO = SCALE / math.log(2.0)
MESH = pl.DeviceIdType.MESH

PAIRS = (
    ((0, 3), (3, 0)),
    ((1, 0), (0, 1)),
    ((3, 3), (0, 2)),
    ((2, 0), (3, 1)),
    ((3, 2), (1, 1)),
    ((1, 3), (2, 3)),
    ("pred", (2, 1)),
    ((1, 2), (2, 2)),
)
PLAN = (
    (("swap", "B"), ("high", 3), ("high", 1), ("swap", "A"), ("B", 0, 1), ("B", 0, 3)),
    (("low", 3), ("F", 3), ("F", 1), ("high", 2)),
    (),
    (("A", 3, 3), ("low", 1)),
    (),
    (("B", 3, 3), ("send back",), ("B", 0, 2), ("B", 3, 1), ("A", 1, 3), ("A", 3, 1), ("low", 2)),
    (),
    (("F", 2),),
    (("A", 3, 2), ("B", 1, 1)),
    (("A", 1, 1), ("B", 3, 2), ("B", 1, 3)),
    (),
    (("A", 1, 2), ("A", 2, 3), ("B", 2, 3), ("pred",), ("B", 2, 1)),
    (),
    (("B", 1, 2), ("A", 2, 1)),
    (("A", 2, 2),),
    (("B", 2, 2),),
    (),
)

SLOT = {block: slot for slot, block in enumerate(block for pair in PAIRS for block in pair)}
PRED = SLOT["pred"]
SWAP, OWN = 16, 17
SPARE = {1: 18, 2: 19, 3: 20}
PARTS = {"A": (0, SHARE), "B": (SHARE, ROWS - SHARE), "F": (0, ROWS)}
GOT = {
    name: number
    for number, name in enumerate(
        [("swap", "A"), ("swap", "B"), ("pred",)]
        + [(kind, dx) for kind in ("high", "low") for dx in (1, 2, 3)]
        + [("F", dy) for dy in (1, 2, 3)]
        + [("B", 0, dx) for dx in (1, 2, 3)]
        + [(part, dy, dx) for part in "AB" for dy in (1, 2, 3) for dx in (1, 2, 3)]
    )
}
SENDS = 80


def body(lengths, queries, keys, values, attended, log_mass, kv, qa, acc, top, scores, weights, fade, feats, turned, docs, local, sent, got):
    here = lax.axis_index("ctx")
    z, y, x = here // 16, here // 4 % 4, here % 4
    right, left = z * 16 + y * 4 + (x + 1) % 4, z * 16 + y * 4 + (x + 3) % 4
    down, up = z * 16 + (y + 1) % 4 * 4 + x, z * 16 + (y + 3) % 4 * 4 + x
    other = (1 - z) * 16 + y * 4 + x
    middle_x = (x == 1) | (x == 2)
    middle_y = (y == 1) | (y == 2)
    edge_x = ~middle_x
    high_to = {
        "right": (x < 3) | (z == 0),
        "left": (x == 0) | (z == 0),
        "down": (y < 3) | (z == 0),
        "up": (y == 0) | (z == 0),
    }

    own_copies = [
        pltpu.make_async_copy(keys, kv.at[OWN // 2, 0, pl.ds(ROWS, ROWS)], local.at[0]),
        pltpu.make_async_copy(values, kv.at[OWN // 2, 1, pl.ds(ROWS, ROWS)], local.at[1]),
    ]
    query_copies = [
        pltpu.make_async_copy(
            queries.at[:, pl.ds(head * HD, HD)], qa.at[pl.ds(head * ROWS, ROWS), pl.ds(0, HD)], local.at[2 + head]
        )
        for head in range(QH)
    ]
    for copy in own_copies + query_copies:
        copy.start()
    barrier = pltpu.get_barrier_semaphore()
    for neighbour in (left, right, up, down, other):
        pl.semaphore_signal(barrier, inc=1, device_id={"ctx": neighbour}, device_id_type=MESH)
    pl.semaphore_wait(barrier, 5)
    for copy in own_copies:
        copy.wait()

    def held(slot, part):
        first, rows = PARTS[part]
        start = slot % 2 * ROWS + first
        return kv.at[slot // 2, :, pl.ds(start if isinstance(slot, int) else pl.multiple_of(start, 64), rows)]

    started = {}

    def push(name, part, source, slot, to, signal, when=None):
        def copy():
            return pltpu.make_async_remote_copy(
                src_ref=held(source, part),
                dst_ref=held(slot, part),
                send_sem=sent.at[number],
                recv_sem=got.at[GOT[signal]],
                device_id={"ctx": to},
                device_id_type=MESH,
            )

        number = started[name][0] if name in started else len(started)
        always = name in started or when is None
        started[name] = (number, part, None if always else when)
        if when is None:
            copy().start()
        else:
            pl.when(when)(lambda: copy().start())

    def arrive(signal, part):
        pltpu.make_async_remote_copy(
            src_ref=held(OWN, part),
            dst_ref=held(SWAP, part),
            send_sem=sent.at[0],
            recv_sem=got.at[GOT[signal]],
            device_id={"ctx": other},
            device_id_type=MESH,
        ).wait_recv()

    def row_slot(high, at_z, at_x, dx):
        needed = ((at_x + dx) % 4 < at_x) | (at_z == 0)
        return jnp.where(needed if high else ~needed, SLOT[0, dx], SPARE[dx])

    def across(dx, high):
        source = row_slot(high, z, x, dx)
        for name, to, dy in (("down", down, 3), ("up", up, 1)):
            when = high_to[name] if high else ~high_to[name]
            push((name, dx), "A", source, SLOT[dy, dx], to, ("A", dy, dx), when)

    def first_x(high):
        for name, to, dx in (("right", right, 3), ("left", left, 1)):
            when = high_to[name] if high else ~high_to[name]
            push((name, "first"), "B", OWN if high else SWAP, SLOT[0, dx], to, ("B", 0, dx), when)

    def first_y(high):
        for name, to, dy in (("down", down, 3), ("up", up, 1)):
            when = high_to[name] if high else ~high_to[name]
            push((name, "first"), "F", OWN if high else SWAP, SLOT[dy, 0], to, ("F", dy), when)

    def take(event):
        kind = event[0]
        if kind == "swap":
            arrive(event, event[1])
            if event[1] == "B":
                first_x(False)
            else:
                first_y(False)
        elif kind == "high":
            dx = event[1]
            arrive(event, "A")
            source = row_slot(True, z, x, dx)
            if dx == 3:
                there = row_slot(True, z, (x + 1) % 4, 2)
                push(("turn", 3), "A", source, there, right, ("high", 2), edge_x)
            if dx == 1:
                there = row_slot(True, z, (x + 3) % 4, 2)
                push(("turn", 1), "A", source, there, left, ("high", 2), edge_x)
            push(("swap", dx), "A", source, row_slot(False, 1 - z, x, dx), other, ("low", dx))
            across(dx, True)
        elif kind == "low":
            arrive(event, "A")
            across(event[1], False)
        elif kind == "F":
            dy = event[1]
            arrive(event, "F")
            push(("on", dy, 3), "B", SLOT[dy, 0], SLOT[dy, 3], right, ("B", dy, 3))
            push(("on", dy, 1), "B", SLOT[dy, 0], SLOT[dy, 1], left, ("B", dy, 1))
            if dy == 3:
                push(("far", 3), "F", SLOT[3, 0], SLOT[2, 0], down, ("F", 2), middle_y)
            if dy == 1:
                push(("far", 1), "F", SLOT[1, 0], SLOT[2, 0], up, ("F", 2), middle_y)
        elif kind == "A":
            _, dy, dx = event
            arrive(event, "A")
            if dy != 2:
                push(("far", dy, dx), "A", SLOT[dy, dx], SLOT[2, dx], down if dy == 3 else up, ("A", 2, dx), middle_y)
        elif kind == "B":
            _, dy, dx = event
            arrive(event, "B")
            if dx != 2:
                when = middle_x if dy in (0, 1) else edge_x
                push(("far x", dy, dx), "B", SLOT[dy, dx], SLOT[dy, 2], right if dx == 3 else left, ("B", dy, 2), when)
        elif kind == "send back":
            push(("pred",), "F", jnp.where(x > 0, SLOT[0, 3], SLOT[3, 3]), PRED, other, ("pred",))
        else:
            arrive(event, "F")

    push(("swap", "B"), "B", OWN, SWAP, other, ("swap", "B"))
    push(("swap", "A"), "A", OWN, SWAP, other, ("swap", "A"))
    push(("right", "row"), "A", OWN, row_slot(True, z, (x + 1) % 4, 3), right, ("high", 3))
    push(("left", "row"), "A", OWN, row_slot(True, z, (x + 3) % 4, 1), left, ("high", 1))
    first_x(True)
    first_y(True)

    lane = lax.broadcasted_iota(jnp.int32, (8, 128), 1)
    begins, ends = jnp.full((8, 128), FAR, jnp.int32), jnp.zeros((8, 128), jnp.int32)
    total = jnp.int32(0)
    for doc in range(DOCS):
        begins = jnp.where(lane == doc, total, begins)
        total = total + lengths[doc]
        ends = jnp.where(lane == doc, total, ends)
    docs[0:8] = begins
    docs[8:16] = ends

    def inside(first):
        place = first + lax.broadcasted_iota(jnp.int32, (ROWS, 128), 0)
        return (place >= docs[0:1]) & (place < docs[8:9])

    for copy in query_copies:
        copy.wait()
    hide = jnp.where(inside(here * ROWS), -HIDE, 0.0).astype(jnp.bfloat16)
    for head in range(QH):
        qa[head * ROWS : (head + 1) * ROWS, HD:] = hide
    top[...] = jnp.full(top.shape, -1e30, jnp.float32)
    acc[...] = jnp.zeros(acc.shape, jnp.float32)
    turned[:, HD:, :] = jnp.ones((2, DEPTH - HD, PAIR), jnp.bfloat16)

    def first_of(block):
        if block == OWN:
            return here * ROWS
        if block == SWAP:
            return jnp.where(z == 1, (here - 16) * ROWS, FAR)
        if block == "pred":
            return jnp.where((z == 1) & (here > 16), (here - 17) * ROWS, FAR)
        dy, dx = block
        column = (y + dy) % 4 * 4 + (x + dx) % 4
        before = column < here % 16
        return jnp.where(before, z * 16 + column, jnp.where(z == 1, column, FAR // ROWS)) * ROWS

    def look(block, half):
        feats[half * ROWS : (half + 1) * ROWS] = jnp.where(inside(first_of(block)), 0.0, 1.0).astype(jnp.bfloat16)

    def score(buffer, key_part, columns):
        scores[buffer, 0 : key_part.shape[0]] = lax.dot_general(
            key_part, qa[columns], (((1,), (1,)), ((), ())), preferred_element_type=jnp.float32
        )

    def soften(buffer, width, first_column, reach=None):
        for lanes in range(0, ROWS, 128):
            at = slice(lanes, lanes + 128)
            columns = pl.ds(pl.multiple_of(first_column + lanes, 128), 128)
            raw = scores[buffer, 0:width, at]
            if reach is not None:
                key = lax.broadcasted_iota(jnp.int32, raw.shape, 0)
                raw = jnp.where(key <= lanes + reach + lax.broadcasted_iota(jnp.int32, raw.shape, 1), raw, -1e30)
                scores[buffer, 0:width, at] = raw
            raw = raw.reshape(width // 8, 8, 128)
            most = jnp.max(jnp.max(raw, axis=0), axis=0, keepdims=True)
            before = top[:, columns]
            now = jnp.maximum(before, jnp.broadcast_to(most, (8, 128)))
            top[:, columns] = now
            fade[buffer, :, at] = jnp.exp2((before - now) * TO_TWO)
            for first in range(0, width, 256):
                part = scores[buffer, first : first + 256, at].reshape(32, 8, 128)
                part = jnp.exp2((part - now[None]) * TO_TWO).reshape(256, 128)
                weights[buffer, first : first + 256, at] = part.astype(jnp.bfloat16)

    def mix(buffer, width, value_part, columns):
        more = jnp.dot(value_part, weights[buffer, 0:width], preferred_element_type=jnp.float32)
        faded = acc[:, columns].reshape(DEPTH // 8, 8, ROWS) * fade[buffer][None]
        acc[:, columns] = faded.reshape(DEPTH, ROWS) + more

    def single(number, nothing):
        @pl.when(number == 0)
        def _():
            look(OWN, 0)

        @pl.when(number == 1)
        def _():
            for event in PLAN[0]:
                take(event)
            look(SWAP, 0)

        rows = pl.ds(pl.multiple_of((1 - number) * ROWS, ROWS), ROWS)
        turned[0, 0:HD, 0:ROWS] = kv[SWAP // 2, 1, rows].T
        reach = jnp.where(number == 0, 0, ROWS)
        key_part = jnp.concatenate([kv[SWAP // 2, 0, rows], feats[0:ROWS]], 1)
        value_part = turned[0, :, 0:ROWS]
        columns = [slice(head * ROWS, (head + 1) * ROWS) for head in range(QH)]
        score(0, key_part, columns[0])
        for head in range(QH):
            if head + 1 < QH:
                score((head + 1) % 2, key_part, columns[head + 1])
            if head > 0:
                mix((head - 1) % 2, ROWS, value_part, columns[head - 1])
            soften(head % 2, ROWS, head * ROWS, reach)
        mix(1, ROWS, value_part, columns[QH - 1])
        return nothing

    lax.fori_loop(0, 2, single, 0)

    scores[1] = jnp.full((PAIR, ROWS), LOWEST, jnp.float32)
    weights[0] = jnp.zeros((PAIR, ROWS), jnp.bfloat16)
    fade[0] = jnp.ones((8, ROWS), jnp.float32)

    def stage(number, nothing):
        pair, half = number // 2, number % 2

        def prepare(which):
            for event in PLAN[1 + which]:
                take(event)
            if which % 2 == 0:
                for side in range(2):
                    look(PAIRS[which // 2][side], side)

        for group in range(0, 16, 4):

            @pl.when((number >= group) & (number < group + 4))
            def _():
                for which in range(group, group + 4):
                    if PLAN[1 + which] or which % 2 == 0:
                        pl.when(number == which)(lambda: prepare(which))

        @pl.when(half == 0)
        def _():
            turned[pair % 2, 0:HD] = kv[pair, 1].T

        at = lambda first: pl.ds(pl.multiple_of(first, ROWS), ROWS)
        now_0, now_1 = half * PAIR, half * PAIR + ROWS
        old_0, old_1 = (1 - half) * PAIR, (1 - half) * PAIR + ROWS
        key_part = jnp.concatenate([kv[pair, 0], feats[...]], 1)
        value_part = turned[jnp.maximum(number - 1, 0) // 2 % 2]
        score(0, key_part, at(now_0))
        mix(0, PAIR, value_part, at(old_0))
        soften(1, PAIR, old_1)
        score(1, key_part, at(now_1))
        mix(1, PAIR, value_part, at(old_1))
        soften(0, PAIR, now_0)
        return nothing

    lax.fori_loop(0, 16, stage, 0)

    mix(0, PAIR, turned[1], slice(2 * ROWS, 3 * ROWS))
    soften(1, PAIR, 3 * ROWS)
    mix(1, PAIR, turned[1], slice(3 * ROWS, 4 * ROWS))

    for head in range(QH):
        columns = slice(head * ROWS, (head + 1) * ROWS)
        mass = acc[HD : HD + 1, columns]
        attended[:, head * HD : (head + 1) * HD] = (acc[0:HD, columns] / mass).T.astype(jnp.bfloat16)
        log_mass[head : head + 1, :] = top[0:1, columns] * SCALE + jnp.log(mass)

    for number, part, when in started.values():

        def finish():
            pltpu.make_async_remote_copy(
                src_ref=held(OWN, part),
                dst_ref=held(SWAP, part),
                send_sem=sent.at[number],
                recv_sem=got.at[0],
                device_id={"ctx": other},
                device_id_type=MESH,
            ).wait_send()

        if when is None:
            finish()
        else:
            pl.when(when)(finish)


def on_device(lengths, queries, key_rows, values):
    vmem = pl.BlockSpec(memory_space=pltpu.VMEM)
    hbm = pl.BlockSpec(memory_space=pl.ANY)
    return pl.pallas_call(
        body,
        out_shape=(
            jax.ShapeDtypeStruct((ROWS, QH * HD), jnp.bfloat16),
            jax.ShapeDtypeStruct((QH, ROWS), jnp.float32),
        ),
        in_specs=[pl.BlockSpec(memory_space=pltpu.SMEM), hbm, hbm, hbm],
        out_specs=(vmem, vmem),
        scratch_shapes=[
            pltpu.VMEM((11, 2, PAIR, HD), jnp.bfloat16),
            pltpu.VMEM((QH * ROWS, 2 * HD), jnp.bfloat16),
            pltpu.VMEM((DEPTH, QH * ROWS), jnp.float32),
            pltpu.VMEM((8, QH * ROWS), jnp.float32),
            pltpu.VMEM((2, PAIR, ROWS), jnp.float32),
            pltpu.VMEM((2, PAIR, ROWS), jnp.bfloat16),
            pltpu.VMEM((2, 8, ROWS), jnp.float32),
            pltpu.VMEM((PAIR, HD), jnp.bfloat16),
            pltpu.VMEM((2, DEPTH, PAIR), jnp.bfloat16),
            pltpu.VMEM((16, 128), jnp.int32),
            pltpu.SemaphoreType.DMA((2 + QH,)),
            pltpu.SemaphoreType.DMA((SENDS,)),
            pltpu.SemaphoreType.DMA((len(GOT),)),
        ],
        compiler_params=pltpu.CompilerParams(collective_id=0, has_side_effects=True, vmem_limit_bytes=56 << 20),
    )(lengths, queries, key_rows, values)


def solution(mesh):
    in_specs = (
        P("batch"),
        P(("batch", "ctx"), None),
        P(("batch", "ctx"), None),
        P(("batch", "ctx"), None),
    )
    out_specs = (P(("batch", "ctx"), None), P(None, ("batch", "ctx")))
    step = jax.shard_map(on_device, mesh=mesh, in_specs=in_specs, out_specs=out_specs, check_vma=False)

    def run(*args):
        with jax.sharding.use_abstract_mesh(mesh.abstract_mesh):
            return step(*args)

    return run
```

```python
import math

import jax
import jax.numpy as jnp
from jax import lax
from jax.experimental import pallas as pl
from jax.experimental.pallas import tpu as pltpu
from jax.sharding import PartitionSpec as P

QH = 4
HD = 128
DOCS = 16
ROWS = 512
PAIR = 2 * ROWS
SHARE = 192
DEPTH = HD + 16
FAR = 1 << 20
HIDE = float(2**20)
LOWEST = -3e38
SCALE = 1.0 / math.sqrt(HD)
TO_TWO = SCALE / math.log(2.0)
MESH = pl.DeviceIdType.MESH

PAIRS = (
    ((0, 3), (3, 0)),
    ((1, 0), (0, 1)),
    ((3, 3), (0, 2)),
    ((2, 0), (3, 1)),
    ((3, 2), (1, 1)),
    ((1, 3), (2, 3)),
    ("pred", (2, 1)),
    ((1, 2), (2, 2)),
)
PLAN = (
    (("swap", "B"), ("high", 3), ("high", 1), ("swap", "A"), ("B", 0, 1), ("B", 0, 3)),
    (("low", 3), ("F", 3), ("F", 1), ("high", 2)),
    (),
    (("A", 3, 3), ("low", 1)),
    (),
    (("B", 3, 3), ("send back",), ("B", 0, 2), ("B", 3, 1), ("A", 1, 3), ("A", 3, 1), ("low", 2)),
    (),
    (("F", 2),),
    (("A", 3, 2), ("B", 1, 1)),
    (("A", 1, 1), ("B", 3, 2), ("B", 1, 3)),
    (),
    (("A", 1, 2), ("A", 2, 3), ("B", 2, 3), ("pred",), ("B", 2, 1)),
    (),
    (("B", 1, 2), ("A", 2, 1)),
    (("A", 2, 2),),
    (("B", 2, 2),),
    (),
)

SLOT = {block: slot for slot, block in enumerate(block for pair in PAIRS for block in pair)}
PRED = SLOT["pred"]
SWAP, OWN = 16, 17
SPARE = {1: 18, 2: 19, 3: 20}
PARTS = {"A": (0, SHARE), "B": (SHARE, ROWS - SHARE), "F": (0, ROWS)}
GOT = {
    name: number
    for number, name in enumerate(
        [("swap", "A"), ("swap", "B"), ("pred",)]
        + [(kind, dx) for kind in ("high", "low") for dx in (1, 2, 3)]
        + [("F", dy) for dy in (1, 2, 3)]
        + [("B", 0, dx) for dx in (1, 2, 3)]
        + [(part, dy, dx) for part in "AB" for dy in (1, 2, 3) for dx in (1, 2, 3)]
    )
}
SENDS = 80


def body(lengths, queries, keys, values, attended, log_mass, kv, qa, acc, top, scores, weights, fade, peak, feats, turned, docs, local, sent, got):
    here = lax.axis_index("ctx")
    z, y, x = here // 16, here // 4 % 4, here % 4
    right, left = z * 16 + y * 4 + (x + 1) % 4, z * 16 + y * 4 + (x + 3) % 4
    down, up = z * 16 + (y + 1) % 4 * 4 + x, z * 16 + (y + 3) % 4 * 4 + x
    other = (1 - z) * 16 + y * 4 + x
    middle_x = (x == 1) | (x == 2)
    middle_y = (y == 1) | (y == 2)
    edge_x = ~middle_x
    high_to = {
        "right": (x < 3) | (z == 0),
        "left": (x == 0) | (z == 0),
        "down": (y < 3) | (z == 0),
        "up": (y == 0) | (z == 0),
    }

    own_copies = [
        pltpu.make_async_copy(keys, kv.at[OWN // 2, 0, pl.ds(ROWS, ROWS)], local.at[0]),
        pltpu.make_async_copy(values, kv.at[OWN // 2, 1, pl.ds(ROWS, ROWS)], local.at[1]),
    ]
    query_copies = [
        pltpu.make_async_copy(
            queries.at[:, pl.ds(head * HD, HD)], qa.at[pl.ds(head * ROWS, ROWS), pl.ds(0, HD)], local.at[2 + head]
        )
        for head in range(QH)
    ]
    for copy in own_copies + query_copies:
        copy.start()
    barrier = pltpu.get_barrier_semaphore()
    for neighbour in (left, right, up, down, other):
        pl.semaphore_signal(barrier, inc=1, device_id={"ctx": neighbour}, device_id_type=MESH)
    pl.semaphore_wait(barrier, 5)
    for copy in own_copies:
        copy.wait()

    def held(slot, part):
        first, rows = PARTS[part]
        start = slot % 2 * ROWS + first
        return kv.at[slot // 2, :, pl.ds(start if isinstance(slot, int) else pl.multiple_of(start, 64), rows)]

    started = {}

    def push(name, part, source, slot, to, signal, when=None):
        def copy():
            return pltpu.make_async_remote_copy(
                src_ref=held(source, part),
                dst_ref=held(slot, part),
                send_sem=sent.at[number],
                recv_sem=got.at[GOT[signal]],
                device_id={"ctx": to},
                device_id_type=MESH,
            )

        number = started[name][0] if name in started else len(started)
        always = name in started or when is None
        started[name] = (number, part, None if always else when)
        if when is None:
            copy().start()
        else:
            pl.when(when)(lambda: copy().start())

    def arrive(signal, part):
        pltpu.make_async_remote_copy(
            src_ref=held(OWN, part),
            dst_ref=held(SWAP, part),
            send_sem=sent.at[0],
            recv_sem=got.at[GOT[signal]],
            device_id={"ctx": other},
            device_id_type=MESH,
        ).wait_recv()

    def row_slot(high, at_z, at_x, dx):
        needed = ((at_x + dx) % 4 < at_x) | (at_z == 0)
        return jnp.where(needed if high else ~needed, SLOT[0, dx], SPARE[dx])

    def across(dx, high):
        source = row_slot(high, z, x, dx)
        for name, to, dy in (("down", down, 3), ("up", up, 1)):
            when = high_to[name] if high else ~high_to[name]
            push((name, dx), "A", source, SLOT[dy, dx], to, ("A", dy, dx), when)

    def first_x(high):
        for name, to, dx in (("right", right, 3), ("left", left, 1)):
            when = high_to[name] if high else ~high_to[name]
            push((name, "first"), "B", OWN if high else SWAP, SLOT[0, dx], to, ("B", 0, dx), when)

    def first_y(high):
        for name, to, dy in (("down", down, 3), ("up", up, 1)):
            when = high_to[name] if high else ~high_to[name]
            push((name, "first"), "F", OWN if high else SWAP, SLOT[dy, 0], to, ("F", dy), when)

    def take(event):
        kind = event[0]
        if kind == "swap":
            arrive(event, event[1])
            if event[1] == "B":
                first_x(False)
            else:
                first_y(False)
        elif kind == "high":
            dx = event[1]
            arrive(event, "A")
            source = row_slot(True, z, x, dx)
            if dx == 3:
                there = row_slot(True, z, (x + 1) % 4, 2)
                push(("turn", 3), "A", source, there, right, ("high", 2), edge_x)
            if dx == 1:
                there = row_slot(True, z, (x + 3) % 4, 2)
                push(("turn", 1), "A", source, there, left, ("high", 2), edge_x)
            push(("swap", dx), "A", source, row_slot(False, 1 - z, x, dx), other, ("low", dx))
            across(dx, True)
        elif kind == "low":
            arrive(event, "A")
            across(event[1], False)
        elif kind == "F":
            dy = event[1]
            arrive(event, "F")
            push(("on", dy, 3), "B", SLOT[dy, 0], SLOT[dy, 3], right, ("B", dy, 3))
            push(("on", dy, 1), "B", SLOT[dy, 0], SLOT[dy, 1], left, ("B", dy, 1))
            if dy == 3:
                push(("far", 3), "F", SLOT[3, 0], SLOT[2, 0], down, ("F", 2), middle_y)
            if dy == 1:
                push(("far", 1), "F", SLOT[1, 0], SLOT[2, 0], up, ("F", 2), middle_y)
        elif kind == "A":
            _, dy, dx = event
            arrive(event, "A")
            if dy != 2:
                push(("far", dy, dx), "A", SLOT[dy, dx], SLOT[2, dx], down if dy == 3 else up, ("A", 2, dx), middle_y)
        elif kind == "B":
            _, dy, dx = event
            arrive(event, "B")
            if dx != 2:
                when = middle_x if dy in (0, 1) else edge_x
                push(("far x", dy, dx), "B", SLOT[dy, dx], SLOT[dy, 2], right if dx == 3 else left, ("B", dy, 2), when)
        elif kind == "send back":
            push(("pred",), "F", jnp.where(x > 0, SLOT[0, 3], SLOT[3, 3]), PRED, other, ("pred",))
        else:
            arrive(event, "F")

    push(("swap", "B"), "B", OWN, SWAP, other, ("swap", "B"))
    push(("swap", "A"), "A", OWN, SWAP, other, ("swap", "A"))
    push(("right", "row"), "A", OWN, row_slot(True, z, (x + 1) % 4, 3), right, ("high", 3))
    push(("left", "row"), "A", OWN, row_slot(True, z, (x + 3) % 4, 1), left, ("high", 1))
    first_x(True)
    first_y(True)

    lane = lax.broadcasted_iota(jnp.int32, (8, 128), 1)
    begins, ends = jnp.full((8, 128), FAR, jnp.int32), jnp.zeros((8, 128), jnp.int32)
    total = jnp.int32(0)
    for doc in range(DOCS):
        begins = jnp.where(lane == doc, total, begins)
        total = total + lengths[doc]
        ends = jnp.where(lane == doc, total, ends)
    docs[0:8] = begins
    docs[8:16] = ends

    def inside(first):
        place = first + lax.broadcasted_iota(jnp.int32, (ROWS, 128), 0)
        return (place >= docs[0:1]) & (place < docs[8:9])

    for copy in query_copies:
        copy.wait()
    hide = jnp.where(inside(here * ROWS), -HIDE, 0.0).astype(jnp.bfloat16)
    for head in range(QH):
        qa[head * ROWS : (head + 1) * ROWS, HD:] = hide
    top[...] = jnp.full(top.shape, -1e30, jnp.float32)
    acc[...] = jnp.zeros(acc.shape, jnp.float32)
    turned[:, HD:, :] = jnp.ones((2, DEPTH - HD, PAIR), jnp.bfloat16)

    def first_of(block):
        if block == OWN:
            return here * ROWS
        if block == SWAP:
            return jnp.where(z == 1, (here - 16) * ROWS, FAR)
        if block == "pred":
            return jnp.where((z == 1) & (here > 16), (here - 17) * ROWS, FAR)
        dy, dx = block
        column = (y + dy) % 4 * 4 + (x + dx) % 4
        before = column < here % 16
        return jnp.where(before, z * 16 + column, jnp.where(z == 1, column, FAR // ROWS)) * ROWS

    def look(block, pair, half):
        seen = inside(first_of(block))
        feats[pair, half * ROWS : (half + 1) * ROWS] = jnp.where(seen, 0.0, 1.0).astype(jnp.bfloat16)

    def score(buffer, key_part, columns):
        raw = lax.dot_general(key_part, qa[columns], (((1,), (1,)), ((), ())), preferred_element_type=jnp.float32)
        scores[buffer, 0 : key_part.shape[0]] = raw
        peak[buffer] = jnp.max(raw.reshape(-1, 8, ROWS), axis=0)

    def soften(buffer, width, first_column, reach=None):
        for lanes in range(0, ROWS, 128):
            at = slice(lanes, lanes + 128)
            columns = pl.ds(pl.multiple_of(first_column + lanes, 128), 128)
            raw = scores[buffer, 0:width, at] if reach is not None else None
            if reach is not None:
                key = lax.broadcasted_iota(jnp.int32, raw.shape, 0)
                raw = jnp.where(key <= lanes + reach + lax.broadcasted_iota(jnp.int32, raw.shape, 1), raw, -1e30)
                scores[buffer, 0:width, at] = raw
            most = peak[buffer, :, at] if raw is None else jnp.max(raw.reshape(width // 8, 8, 128), axis=0)
            most = jnp.max(most, axis=0, keepdims=True)
            before = top[:, columns]
            now = jnp.maximum(before, jnp.broadcast_to(most, (8, 128)))
            top[:, columns] = now
            fade[buffer, :, at] = jnp.exp2((before - now) * TO_TWO)
            for first in range(0, width, 256):
                part = scores[buffer, first : first + 256, at].reshape(32, 8, 128)
                part = jnp.exp2((part - now[None]) * TO_TWO).reshape(256, 128)
                weights[buffer, first : first + 256, at] = part.astype(jnp.bfloat16)

    def mix(buffer, width, value_part, columns):
        more = jnp.dot(value_part, weights[buffer, 0:width], preferred_element_type=jnp.float32)
        faded = acc[:, columns].reshape(DEPTH // 8, 8, ROWS) * fade[buffer][None]
        acc[:, columns] = faded.reshape(DEPTH, ROWS) + more

    def single(slot, reach):
        rows = pl.ds(slot % 2 * ROWS, ROWS)
        turned[0, 0:HD, 0:ROWS] = kv[slot // 2, 1, rows].T
        key_part = jnp.concatenate([kv[slot // 2, 0, rows], feats[len(PAIRS), rows]], 1)
        value_part = turned[0, :, 0:ROWS]
        columns = [slice(head * ROWS, (head + 1) * ROWS) for head in range(QH)]
        score(0, key_part, columns[0])
        for head in range(QH):
            if head + 1 < QH:
                score((head + 1) % 2, key_part, columns[head + 1])
            if head > 0:
                mix((head - 1) % 2, ROWS, value_part, columns[head - 1])
            soften(head % 2, ROWS, head * ROWS, reach)
        mix(1, ROWS, value_part, columns[QH - 1])

    look(OWN, len(PAIRS), OWN % 2)
    single(OWN, 0)
    look(SWAP, len(PAIRS), SWAP % 2)
    for number, pair in enumerate(PAIRS):
        for half in range(2):
            look(pair[half], number, half)
    for event in PLAN[0]:
        take(event)
    single(SWAP, None)

    scores[1] = jnp.full((PAIR, ROWS), LOWEST, jnp.float32)
    weights[0] = jnp.zeros((PAIR, ROWS), jnp.bfloat16)
    fade[0] = jnp.ones((8, ROWS), jnp.float32)
    peak[1] = jnp.full((8, ROWS), LOWEST, jnp.float32)

    def stage(number, nothing):
        pair, half = number // 2, number % 2

        def prepare(which):
            for event in PLAN[1 + which]:
                take(event)

        for group in range(0, 16, 4):

            @pl.when((number >= group) & (number < group + 4))
            def _():
                for which in range(group, group + 4):
                    if PLAN[1 + which]:
                        pl.when(number == which)(lambda: prepare(which))

        @pl.when(half == 0)
        def _():
            turned[pair % 2, 0:HD] = kv[pair, 1].T

        at = lambda first: pl.ds(pl.multiple_of(first, ROWS), ROWS)
        now_0, now_1 = half * PAIR, half * PAIR + ROWS
        old_0, old_1 = (1 - half) * PAIR, (1 - half) * PAIR + ROWS

        @pl.when(here >= 0)
        def _():
            soften(1, PAIR, old_1)
            score(0, jnp.concatenate([kv[pair, 0], feats[pair]], 1), at(now_0))
            mix(0, PAIR, turned[jnp.maximum(number - 1, 0) // 2 % 2], at(old_0))

        @pl.when(here < 32)
        def _():
            soften(0, PAIR, now_0)
            score(1, jnp.concatenate([kv[pair, 0], feats[pair]], 1), at(now_1))
            mix(1, PAIR, turned[jnp.maximum(number - 1, 0) // 2 % 2], at(old_1))

        return nothing

    lax.fori_loop(0, 16, stage, 0)

    mix(0, PAIR, turned[1], slice(2 * ROWS, 3 * ROWS))
    soften(1, PAIR, 3 * ROWS)
    mix(1, PAIR, turned[1], slice(3 * ROWS, 4 * ROWS))

    for head in range(QH):
        columns = slice(head * ROWS, (head + 1) * ROWS)
        mass = acc[HD : HD + 1, columns]
        attended[:, head * HD : (head + 1) * HD] = (acc[0:HD, columns] / mass).T.astype(jnp.bfloat16)
        log_mass[head : head + 1, :] = top[0:1, columns] * SCALE + jnp.log(mass)

    for number, part, when in started.values():

        def finish():
            pltpu.make_async_remote_copy(
                src_ref=held(OWN, part),
                dst_ref=held(SWAP, part),
                send_sem=sent.at[number],
                recv_sem=got.at[0],
                device_id={"ctx": other},
                device_id_type=MESH,
            ).wait_send()

        if when is None:
            finish()
        else:
            pl.when(when)(finish)


def on_device(lengths, queries, key_rows, values):
    vmem = pl.BlockSpec(memory_space=pltpu.VMEM)
    hbm = pl.BlockSpec(memory_space=pltpu.HBM)
    return pl.pallas_call(
        body,
        out_shape=(
            jax.ShapeDtypeStruct((ROWS, QH * HD), jnp.bfloat16),
            jax.ShapeDtypeStruct((QH, ROWS), jnp.float32),
        ),
        in_specs=[pl.BlockSpec(memory_space=pltpu.SMEM), hbm, hbm, hbm],
        out_specs=(vmem, vmem),
        scratch_shapes=[
            pltpu.VMEM((11, 2, PAIR, HD), jnp.bfloat16),
            pltpu.VMEM((QH * ROWS, 2 * HD), jnp.bfloat16),
            pltpu.VMEM((DEPTH, QH * ROWS), jnp.float32),
            pltpu.VMEM((8, QH * ROWS), jnp.float32),
            pltpu.VMEM((2, PAIR, ROWS), jnp.float32),
            pltpu.VMEM((2, PAIR, ROWS), jnp.bfloat16),
            pltpu.VMEM((2, 8, ROWS), jnp.float32),
            pltpu.VMEM((2, 8, ROWS), jnp.float32),
            pltpu.VMEM((len(PAIRS) + 1, PAIR, HD), jnp.bfloat16),
            pltpu.VMEM((2, DEPTH, PAIR), jnp.bfloat16),
            pltpu.VMEM((16, 128), jnp.int32),
            pltpu.SemaphoreType.DMA((2 + QH,)),
            pltpu.SemaphoreType.DMA((SENDS,)),
            pltpu.SemaphoreType.DMA((len(GOT),)),
        ],
        compiler_params=pltpu.CompilerParams(collective_id=0, has_side_effects=True, vmem_limit_bytes=56 << 20),
    )(lengths, queries, key_rows, values)


def solution(mesh):
    in_specs = (
        P("batch"),
        P(("batch", "ctx"), None),
        P(("batch", "ctx"), None),
        P(("batch", "ctx"), None),
    )
    out_specs = (P(("batch", "ctx"), None), P(None, ("batch", "ctx")))
    step = jax.shard_map(on_device, mesh=mesh, in_specs=in_specs, out_specs=out_specs, check_vma=False)

    def run(*args):
        with jax.sharding.use_abstract_mesh(mesh.abstract_mesh):
            return step(*args)

    return run
```

```python
import math

import jax
import jax.numpy as jnp
from jax import lax
from jax.experimental import pallas as pl
from jax.experimental.pallas import tpu as pltpu
from jax.sharding import PartitionSpec as P

QH = 4
HD = 128
DOCS = 16
ROWS = 512
PAIR = 2 * ROWS
SHARE = 192
DEPTH = HD + 16
FAR = 1 << 20
HIDE = float(2**20)
LOWEST = -3e38
SCALE = 1.0 / math.sqrt(HD)
TO_TWO = SCALE / math.log(2.0)
MESH = pl.DeviceIdType.MESH

PAIRS = (
    ((0, 3), (3, 0)),
    ((1, 0), (0, 1)),
    ((3, 3), (0, 2)),
    ((2, 0), (3, 1)),
    ((3, 2), (1, 1)),
    ((1, 3), (2, 3)),
    ("pred", (2, 1)),
    ((1, 2), (2, 2)),
)
PLAN = (
    (("swap", "B"), ("high", 3), ("high", 1), ("swap", "A"), ("B", 0, 1), ("B", 0, 3)),
    (("low", 3), ("F", 3), ("F", 1), ("high", 2)),
    (),
    (("A", 3, 3), ("low", 1)),
    (),
    (("B", 3, 3), ("send back",), ("B", 0, 2), ("B", 3, 1), ("A", 1, 3), ("A", 3, 1), ("low", 2)),
    (),
    (("F", 2),),
    (("A", 3, 2), ("B", 1, 1)),
    (("A", 1, 1), ("B", 3, 2), ("B", 1, 3)),
    (),
    (("A", 1, 2), ("A", 2, 3), ("B", 2, 3), ("pred",), ("B", 2, 1)),
    (),
    (("B", 1, 2), ("A", 2, 1)),
    (("A", 2, 2),),
    (("B", 2, 2),),
    (),
)

SLOT = {block: slot for slot, block in enumerate(block for pair in PAIRS for block in pair)}
PRED = SLOT["pred"]
SWAP, OWN = 16, 17
SPARE = {1: 18, 2: 19, 3: 20}
PARTS = {"A": (0, SHARE), "B": (SHARE, ROWS - SHARE), "F": (0, ROWS)}
GOT = {
    name: number
    for number, name in enumerate(
        [("swap", "A"), ("swap", "B"), ("pred",)]
        + [(kind, dx) for kind in ("high", "low") for dx in (1, 2, 3)]
        + [("F", dy) for dy in (1, 2, 3)]
        + [("B", 0, dx) for dx in (1, 2, 3)]
        + [(part, dy, dx) for part in "AB" for dy in (1, 2, 3) for dx in (1, 2, 3)]
    )
}
SENDS = 80


def body(lengths, queries, keys, values, attended, log_mass, kv, qa, acc, top, scores, weights, fade, peak, feats, turned, docs, local, sent, got):
    here = lax.axis_index("ctx")
    z, y, x = here // 16, here // 4 % 4, here % 4
    right, left = z * 16 + y * 4 + (x + 1) % 4, z * 16 + y * 4 + (x + 3) % 4
    down, up = z * 16 + (y + 1) % 4 * 4 + x, z * 16 + (y + 3) % 4 * 4 + x
    other = (1 - z) * 16 + y * 4 + x
    middle_x = (x == 1) | (x == 2)
    middle_y = (y == 1) | (y == 2)
    edge_x = ~middle_x
    high_to = {
        "right": (x < 3) | (z == 0),
        "left": (x == 0) | (z == 0),
        "down": (y < 3) | (z == 0),
        "up": (y == 0) | (z == 0),
    }

    own_copies = [
        pltpu.make_async_copy(keys, kv.at[OWN // 2, 0, pl.ds(ROWS, ROWS)], local.at[0]),
        pltpu.make_async_copy(values, kv.at[OWN // 2, 1, pl.ds(ROWS, ROWS)], local.at[1]),
    ]
    query_copies = [
        pltpu.make_async_copy(
            queries.at[:, pl.ds(head * HD, HD)], qa.at[pl.ds(head * ROWS, ROWS), pl.ds(0, HD)], local.at[2 + head]
        )
        for head in range(QH)
    ]
    for copy in own_copies + query_copies:
        copy.start()
    barrier = pltpu.get_barrier_semaphore()
    for neighbour in (left, right, up, down, other):
        pl.semaphore_signal(barrier, inc=1, device_id={"ctx": neighbour}, device_id_type=MESH)
    pl.semaphore_wait(barrier, 5)
    for copy in own_copies:
        copy.wait()

    def held(slot, part):
        first, rows = PARTS[part]
        start = slot % 2 * ROWS + first
        return kv.at[slot // 2, :, pl.ds(start if isinstance(slot, int) else pl.multiple_of(start, 64), rows)]

    started = {}

    def push(name, part, source, slot, to, signal, when=None):
        def copy():
            return pltpu.make_async_remote_copy(
                src_ref=held(source, part),
                dst_ref=held(slot, part),
                send_sem=sent.at[number],
                recv_sem=got.at[GOT[signal]],
                device_id={"ctx": to},
                device_id_type=MESH,
            )

        number = started[name][0] if name in started else len(started)
        always = name in started or when is None
        started[name] = (number, part, None if always else when)
        if when is None:
            copy().start()
        else:
            pl.when(when)(lambda: copy().start())

    def arrive(signal, part):
        pltpu.make_async_remote_copy(
            src_ref=held(OWN, part),
            dst_ref=held(SWAP, part),
            send_sem=sent.at[0],
            recv_sem=got.at[GOT[signal]],
            device_id={"ctx": other},
            device_id_type=MESH,
        ).wait_recv()

    def row_slot(high, at_z, at_x, dx):
        needed = ((at_x + dx) % 4 < at_x) | (at_z == 0)
        return jnp.where(needed if high else ~needed, SLOT[0, dx], SPARE[dx])

    def across(dx, high):
        source = row_slot(high, z, x, dx)
        for name, to, dy in (("down", down, 3), ("up", up, 1)):
            when = high_to[name] if high else ~high_to[name]
            push((name, dx), "A", source, SLOT[dy, dx], to, ("A", dy, dx), when)

    def first_x(high):
        for name, to, dx in (("right", right, 3), ("left", left, 1)):
            when = high_to[name] if high else ~high_to[name]
            push((name, "first"), "B", OWN if high else SWAP, SLOT[0, dx], to, ("B", 0, dx), when)

    def first_y(high):
        for name, to, dy in (("down", down, 3), ("up", up, 1)):
            when = high_to[name] if high else ~high_to[name]
            push((name, "first"), "F", OWN if high else SWAP, SLOT[dy, 0], to, ("F", dy), when)

    def take(event):
        kind = event[0]
        if kind == "swap":
            arrive(event, event[1])
            if event[1] == "B":
                first_x(False)
            else:
                first_y(False)
        elif kind == "high":
            dx = event[1]
            arrive(event, "A")
            source = row_slot(True, z, x, dx)
            if dx == 3:
                there = row_slot(True, z, (x + 1) % 4, 2)
                push(("turn", 3), "A", source, there, right, ("high", 2), edge_x)
            if dx == 1:
                there = row_slot(True, z, (x + 3) % 4, 2)
                push(("turn", 1), "A", source, there, left, ("high", 2), edge_x)
            push(("swap", dx), "A", source, row_slot(False, 1 - z, x, dx), other, ("low", dx))
            across(dx, True)
        elif kind == "low":
            arrive(event, "A")
            across(event[1], False)
        elif kind == "F":
            dy = event[1]
            arrive(event, "F")
            push(("on", dy, 3), "B", SLOT[dy, 0], SLOT[dy, 3], right, ("B", dy, 3))
            push(("on", dy, 1), "B", SLOT[dy, 0], SLOT[dy, 1], left, ("B", dy, 1))
            if dy == 3:
                push(("far", 3), "F", SLOT[3, 0], SLOT[2, 0], down, ("F", 2), middle_y)
            if dy == 1:
                push(("far", 1), "F", SLOT[1, 0], SLOT[2, 0], up, ("F", 2), middle_y)
        elif kind == "A":
            _, dy, dx = event
            arrive(event, "A")
            if dy != 2:
                push(("far", dy, dx), "A", SLOT[dy, dx], SLOT[2, dx], down if dy == 3 else up, ("A", 2, dx), middle_y)
        elif kind == "B":
            _, dy, dx = event
            arrive(event, "B")
            if dx != 2:
                when = middle_x if dy in (0, 1) else edge_x
                push(("far x", dy, dx), "B", SLOT[dy, dx], SLOT[dy, 2], right if dx == 3 else left, ("B", dy, 2), when)
        elif kind == "send back":
            push(("pred",), "F", jnp.where(x > 0, SLOT[0, 3], SLOT[3, 3]), PRED, other, ("pred",))
        else:
            arrive(event, "F")

    push(("swap", "B"), "B", OWN, SWAP, other, ("swap", "B"))
    push(("swap", "A"), "A", OWN, SWAP, other, ("swap", "A"))
    push(("right", "row"), "A", OWN, row_slot(True, z, (x + 1) % 4, 3), right, ("high", 3))
    push(("left", "row"), "A", OWN, row_slot(True, z, (x + 3) % 4, 1), left, ("high", 1))
    first_x(True)
    first_y(True)

    lane = lax.broadcasted_iota(jnp.int32, (8, 128), 1)
    begins, ends = jnp.full((8, 128), FAR, jnp.int32), jnp.zeros((8, 128), jnp.int32)
    total = jnp.int32(0)
    for doc in range(DOCS):
        begins = jnp.where(lane == doc, total, begins)
        total = total + lengths[doc]
        ends = jnp.where(lane == doc, total, ends)
    docs[0:8] = begins
    docs[8:16] = ends

    def inside(first):
        place = first + lax.broadcasted_iota(jnp.int32, (ROWS, 128), 0)
        return (place >= docs[0:1]) & (place < docs[8:9])

    for copy in query_copies:
        copy.wait()
    hide = jnp.where(inside(here * ROWS), -HIDE, 0.0).astype(jnp.bfloat16)
    for head in range(QH):
        qa[head * ROWS : (head + 1) * ROWS, HD:] = hide
    top[...] = jnp.full(top.shape, -1e30, jnp.float32)
    acc[...] = jnp.zeros(acc.shape, jnp.float32)
    turned[:, HD:, :] = jnp.ones((2, DEPTH - HD, PAIR), jnp.bfloat16)

    def first_of(block):
        if block == OWN:
            return here * ROWS
        if block == SWAP:
            return jnp.where(z == 1, (here - 16) * ROWS, FAR)
        if block == "pred":
            return jnp.where((z == 1) & (here > 16), (here - 17) * ROWS, FAR)
        dy, dx = block
        column = (y + dy) % 4 * 4 + (x + dx) % 4
        before = column < here % 16
        return jnp.where(before, z * 16 + column, jnp.where(z == 1, column, FAR // ROWS)) * ROWS

    def look(block, pair, half):
        seen = inside(first_of(block))
        feats[pair, half * ROWS : (half + 1) * ROWS] = jnp.where(seen, 0.0, 1.0).astype(jnp.bfloat16)

    def score(buffer, key_part, columns):
        raw = lax.dot_general(key_part, qa[columns], (((1,), (1,)), ((), ())), preferred_element_type=jnp.float32)
        scores[buffer, 0 : key_part.shape[0]] = raw
        peak[buffer] = jnp.max(raw.reshape(-1, 8, ROWS), axis=0)

    def soften(buffer, width, first_column, reach=None):
        for lanes in range(0, ROWS, 128):
            at = slice(lanes, lanes + 128)
            columns = pl.ds(pl.multiple_of(first_column + lanes, 128), 128)
            raw = scores[buffer, 0:width, at] if reach is not None else None
            if reach is not None:
                key = lax.broadcasted_iota(jnp.int32, raw.shape, 0)
                raw = jnp.where(key <= lanes + reach + lax.broadcasted_iota(jnp.int32, raw.shape, 1), raw, -1e30)
                scores[buffer, 0:width, at] = raw
            most = peak[buffer, :, at] if raw is None else jnp.max(raw.reshape(width // 8, 8, 128), axis=0)
            most = jnp.max(most, axis=0, keepdims=True)
            before = top[:, columns]
            now = jnp.maximum(before, jnp.broadcast_to(most, (8, 128)))
            top[:, columns] = now
            fade[buffer, :, at] = jnp.exp2((before - now) * TO_TWO)
            for first in range(0, width, 256):
                part = scores[buffer, first : first + 256, at].reshape(32, 8, 128)
                part = jnp.exp2((part - now[None]) * TO_TWO).reshape(256, 128)
                weights[buffer, first : first + 256, at] = part.astype(jnp.bfloat16)

    def mix(buffer, width, value_part, columns):
        more = jnp.dot(value_part, weights[buffer, 0:width], preferred_element_type=jnp.float32)
        faded = acc[:, columns].reshape(DEPTH // 8, 8, ROWS) * fade[buffer][None]
        acc[:, columns] = faded.reshape(DEPTH, ROWS) + more

    def single(slot, reach):
        rows = pl.ds(slot % 2 * ROWS, ROWS)
        turned[0, 0:HD, 0:ROWS] = kv[slot // 2, 1, rows].T
        key_part = jnp.concatenate([kv[slot // 2, 0, rows], feats[len(PAIRS), rows]], 1)
        value_part = turned[0, :, 0:ROWS]
        columns = [slice(head * ROWS, (head + 1) * ROWS) for head in range(QH)]
        score(0, key_part, columns[0])
        for head in range(QH):
            if head + 1 < QH:
                score((head + 1) % 2, key_part, columns[head + 1])
            if head > 0:
                mix((head - 1) % 2, ROWS, value_part, columns[head - 1])
            soften(head % 2, ROWS, head * ROWS, reach)
        mix(1, ROWS, value_part, columns[QH - 1])

    look(OWN, len(PAIRS), OWN % 2)
    single(OWN, 0)
    look(SWAP, len(PAIRS), SWAP % 2)
    for number, pair in enumerate(PAIRS):
        for half in range(2):
            look(pair[half], number, half)
    for event in PLAN[0]:
        take(event)
    single(SWAP, None)

    scores[1] = jnp.full((PAIR, ROWS), LOWEST, jnp.float32)
    weights[0] = jnp.zeros((PAIR, ROWS), jnp.bfloat16)
    fade[0] = jnp.ones((8, ROWS), jnp.float32)
    peak[1] = jnp.full((8, ROWS), LOWEST, jnp.float32)

    def stage(number, nothing):
        pair, half = number // 2, number % 2

        def prepare(which):
            for event in PLAN[1 + which]:
                take(event)

        for group in range(0, 16, 4):

            @pl.when((number >= group) & (number < group + 4))
            def _():
                for which in range(group, group + 4):
                    if PLAN[1 + which]:
                        pl.when(number == which)(lambda: prepare(which))

        @pl.when(half == 0)
        def _():
            turned[pair % 2, 0:HD] = kv[pair, 1].T

        at = lambda first: pl.ds(pl.multiple_of(first, ROWS), ROWS)
        now_0, now_1 = half * PAIR, half * PAIR + ROWS
        old_0, old_1 = (1 - half) * PAIR, (1 - half) * PAIR + ROWS

        @pl.when(here >= 0)
        def _():
            soften(1, PAIR, old_1)
            score(0, jnp.concatenate([kv[pair, 0], feats[pair]], 1), at(now_0))
            mix(0, PAIR, turned[jnp.maximum(number - 1, 0) // 2 % 2], at(old_0))

        @pl.when(here < 32)
        def _():
            soften(0, PAIR, now_0)
            score(1, jnp.concatenate([kv[pair, 0], feats[pair]], 1), at(now_1))
            mix(1, PAIR, turned[jnp.maximum(number - 1, 0) // 2 % 2], at(old_1))

        return nothing

    lax.fori_loop(0, 16, stage, 0)

    mix(0, PAIR, turned[1], slice(2 * ROWS, 3 * ROWS))
    soften(1, PAIR, 3 * ROWS)
    mix(1, PAIR, turned[1], slice(3 * ROWS, 4 * ROWS))

    for head in range(QH):
        columns = slice(head * ROWS, (head + 1) * ROWS)
        mass = acc[HD : HD + 1, columns]
        attended[:, head * HD : (head + 1) * HD] = (acc[0:HD, columns] * (1.0 / mass)).astype(jnp.bfloat16).T
        log_mass[head : head + 1, :] = top[0:1, columns] * SCALE + jnp.log(mass)

    for number, part, when in started.values():

        def finish():
            pltpu.make_async_remote_copy(
                src_ref=held(OWN, part),
                dst_ref=held(SWAP, part),
                send_sem=sent.at[number],
                recv_sem=got.at[0],
                device_id={"ctx": other},
                device_id_type=MESH,
            ).wait_send()

        if when is None:
            finish()
        else:
            pl.when(when)(finish)


def on_device(lengths, queries, key_rows, values):
    vmem = pl.BlockSpec(memory_space=pltpu.VMEM)
    hbm = pl.BlockSpec(memory_space=pltpu.HBM)
    return pl.pallas_call(
        body,
        out_shape=(
            jax.ShapeDtypeStruct((ROWS, QH * HD), jnp.bfloat16),
            jax.ShapeDtypeStruct((QH, ROWS), jnp.float32),
        ),
        in_specs=[pl.BlockSpec(memory_space=pltpu.SMEM), hbm, hbm, hbm],
        out_specs=(vmem, vmem),
        scratch_shapes=[
            pltpu.VMEM((11, 2, PAIR, HD), jnp.bfloat16),
            pltpu.VMEM((QH * ROWS, 2 * HD), jnp.bfloat16),
            pltpu.VMEM((DEPTH, QH * ROWS), jnp.float32),
            pltpu.VMEM((8, QH * ROWS), jnp.float32),
            pltpu.VMEM((2, PAIR, ROWS), jnp.float32),
            pltpu.VMEM((2, PAIR, ROWS), jnp.bfloat16),
            pltpu.VMEM((2, 8, ROWS), jnp.float32),
            pltpu.VMEM((2, 8, ROWS), jnp.float32),
            pltpu.VMEM((len(PAIRS) + 1, PAIR, HD), jnp.bfloat16),
            pltpu.VMEM((2, DEPTH, PAIR), jnp.bfloat16),
            pltpu.VMEM((16, 128), jnp.int32),
            pltpu.SemaphoreType.DMA((2 + QH,)),
            pltpu.SemaphoreType.DMA((SENDS,)),
            pltpu.SemaphoreType.DMA((len(GOT),)),
        ],
        compiler_params=pltpu.CompilerParams(collective_id=0, has_side_effects=True, vmem_limit_bytes=56 << 20),
    )(lengths, queries, key_rows, values)


def solution(mesh):
    in_specs = (
        P("batch"),
        P(("batch", "ctx"), None),
        P(("batch", "ctx"), None),
        P(("batch", "ctx"), None),
    )
    out_specs = (P(("batch", "ctx"), None), P(None, ("batch", "ctx")))
    step = jax.shard_map(on_device, mesh=mesh, in_specs=in_specs, out_specs=out_specs, check_vma=False)

    def run(*args):
        with jax.sharding.use_abstract_mesh(mesh.abstract_mesh):
            return step(*args)

    return run
```
